32 devices in a mesh: member: 16 (over z, y, x), domain: 2 (over core).
Axes of the slice: x: 2, y: 2, z: 4, core: 2. Of those that a mesh axis runs over, the one named last changes fastest.
Arguments:
- state: bfloat16 [512, 32768], P('member', 'domain'), may hold values from -6 to 6
- predicted: bfloat16 [512, 65536], P('member', 'domain'), may hold values from -6 to 6
- perturbed: bfloat16 [512, 65536], P('member', 'domain'), may hold values from -6 to 6
- obs_weight: float32 [65536], P('domain'), may hold values from 0.3 to 3
- obs_position: int32 [65536], P('domain'), may hold values from 0 to 63
- row_count: int32 [2, 32], P(None, 'member'), may hold values from 256 to 2048
- row_index: int32 [2, 32, 2048], P('domain', 'member'), may hold values from 0 to 2047, as said below
Outputs:
- updated: bfloat16 [512, 32768], P('member', 'domain')
The draws below stay inside these ranges and needn't reach their ends.
Inputs may be any that keep to these rules, and one draw needn't show every extreme that they name: `row_index`: for each block, 2048 distinct rows of its pool; only the first row_count of them are used.
All inputs are finite; a program needn't handle non-finite values.
Results may differ from the reference program's by a relative error of at most 0.0054.
Values may be sent and summed in bfloat16 or wider, within the bound.
A program may use at most 128 MiB of HBM per device.

```python
import math
import jax
import jax.numpy as jnp
from jax import lax

MEMBERS = 512
ROWCAP = 2048
ROWMIN = 256
POOL = 2048
BPD = 2
NS_STEPS = 5
SPAN = 2
TILES = 2
TILE_BLOCKS = 32
NBLOCKS = 64
CELLS = 32768
OBS = 65536


def draw_obs_position(key, part):
    base_block = jnp.arange(OBS, dtype=jnp.int32) // POOL * BPD
    shifted = jax.random.randint(key, (OBS,), -2 * SPAN, BPD + 2 * SPAN, dtype=jnp.int32)
    return jnp.clip(base_block + shifted, 0, NBLOCKS - 1).astype(jnp.int32)


def draw_row_count(key, part):
    levels = jax.random.randint(key, (TILES, TILE_BLOCKS), 0, 1024, dtype=jnp.int32)
    counts = ROWMIN + levels * levels * (ROWCAP - ROWMIN) // (1023 * 1023)
    counts = counts.at[0, 0].set(ROWCAP)
    counts = counts.at[0, 1].set(ROWMIN)
    return counts.astype(jnp.int32)


def draw_row_index(key, part):
    keys = jax.random.split(key, TILES * TILE_BLOCKS)

    def one_list(single_key):
        return jax.random.permutation(single_key, POOL)[:ROWCAP]
    lists = jax.vmap(one_list)(keys)
    return lists.reshape(TILES, TILE_BLOCKS, ROWCAP).astype(jnp.int32)


def steps_of(own_key, extent, cuts, least, largest):
    factor_of, own = 1.0, jax.random.fold_in(own_key, 6)
    for dim, shards_of in cuts:
        draws = jnp.exp(jax.random.uniform(jax.random.fold_in(own, dim), (shards_of,), jnp.float32, least / len(cuts), largest / len(cuts)))
        factor_of = factor_of * jnp.repeat(draws, extent[dim] // shards_of).reshape([-1 if axis == dim else 1 for axis in range(len(extent))])
    return factor_of


def noise(own_key, extent, scale, most, cuts=(), kind=jnp.bfloat16):
    values = jax.random.normal(own_key, extent, jnp.float32) * scale
    if len(cuts) > 0:
        values = steps_of(own_key, extent, cuts, -0.22, 0.18) * values
    return jnp.clip(values, min=-most, max=most).astype(kind)


def setup_inputs(seed: int = 0) -> dict:
    key_list = jax.random.split(jax.random.key(seed), 8)
    state = noise(key_list[0], (MEMBERS, CELLS), 1.0, 6.0, ((0, 16), (1, 2)))
    predicted = noise(key_list[1], (MEMBERS, OBS), 1.0, 6.0, ((0, 16), (1, 2)))
    perturbed = noise(key_list[2], (MEMBERS, OBS), 1.0, 6.0, ((0, 16), (1, 2)))
    obs_weight = jnp.clip(jnp.exp(math.log(3.0) - 2.3025851 * jax.random.uniform(key_list[3], (OBS,), jnp.float32) ** steps_of(key_list[3], (OBS,), ((0, 2),), -0.2, 0.2)), 0.3, 3.0)
    obs_position = draw_obs_position(jax.random.fold_in(key_list[7], 71), 0)
    row_count = draw_row_count(jax.random.fold_in(key_list[7], 71), 0)
    row_index = draw_row_index(jax.random.fold_in(key_list[7], 71), 0)
    return dict(state=state, predicted=predicted, perturbed=perturbed, obs_weight=obs_weight, obs_position=obs_position, row_count=row_count, row_index=row_index)


def scaled_rows(obs_pools, index_list, row_total, position, row_start, length):
    pred_pool, pert_pool, mean_pred, weight_pool, place_pool = obs_pools
    picked = lax.dynamic_slice_in_dim(index_list, row_start, length)
    pred_rows = jnp.take(pred_pool, picked, axis=0).astype(jnp.float32)
    pert_rows = jnp.take(pert_pool, picked, axis=0).astype(jnp.float32)
    offset = (jnp.take(place_pool, picked) - position).astype(jnp.float32) / SPAN
    taper_factor = 1.0 / (1.0 + offset * offset)
    live_rows = row_start + jnp.arange(length, dtype=jnp.int32) < row_total
    factor = jnp.where(live_rows, jnp.take(weight_pool, picked) * taper_factor, 0.0)
    members = pred_pool.shape[1]
    scaled = (factor[:, None] * (pred_rows - jnp.take(mean_pred, picked)[:, None]) / jnp.sqrt(members - 1.0)).astype(jnp.bfloat16)
    innovation = (factor[:, None] * (pert_rows - pred_rows)).astype(jnp.bfloat16)
    return (scaled, innovation)

def newton_inverse(gram_sum):
    members = gram_sum.shape[0]
    identity = jnp.eye(members, dtype=jnp.float32)
    system = identity + gram_sum
    spread = jnp.sqrt(jnp.sum(gram_sum * gram_sum))
    estimate = 2.0 / (2.0 + spread) * identity
    for iteration in range(NS_STEPS):
        product = jnp.dot(system, estimate, precision=lax.Precision.HIGHEST)
        estimate = jnp.dot(estimate, 2.0 * identity - product, precision=lax.Precision.HIGHEST)
    return estimate

def update_block(cell_block, gram_sum, cross_sum):
    members = gram_sum.shape[0]
    inverse = newton_inverse(gram_sum)
    weights = (jnp.dot(inverse, cross_sum, precision=lax.Precision.HIGHEST) / math.sqrt(members - 1.0)).astype(jnp.bfloat16)
    values = cell_block.astype(jnp.float32)
    centred = (values - lax.optimization_barrier(jnp.mean(values, axis=1, keepdims=True))).astype(jnp.bfloat16)
    change = jnp.dot(centred.astype(jnp.float32), weights.astype(jnp.float32), precision=lax.Precision.HIGHEST)
    return (values + change).astype(jnp.bfloat16)

def reference(state, predicted, perturbed, obs_weight, obs_position, row_count, row_index):
    cell_major = state.T
    pred_rows_all = predicted.T
    pert_rows_all = perturbed.T
    members = cell_major.shape[1]
    block_total = row_count.shape[0] * row_count.shape[1]
    counts = row_count.reshape(block_total)
    lists = row_index.reshape(block_total, row_index.shape[2])
    cell_blocks = cell_major.reshape(block_total, cell_major.shape[0] // block_total, members)
    mean_pred = lax.optimization_barrier(jnp.mean(pred_rows_all, axis=1, dtype=jnp.float32))
    obs_pools = (pred_rows_all, pert_rows_all, mean_pred, obs_weight, obs_position)

    def one_block(inputs):
        cell_block, index_list, row_total, number = inputs
        offset_rows = (number // BPD * POOL).astype(jnp.int32)
        scaled, innovation = scaled_rows(obs_pools, index_list + offset_rows, row_total, number, 0, index_list.shape[0])
        scaled_wide = scaled.astype(jnp.float32)
        innov_wide = innovation.astype(jnp.float32)
        gram_sum = jnp.dot(scaled_wide.T, scaled_wide, precision=lax.Precision.HIGHEST)
        cross_sum = jnp.dot(scaled_wide.T, innov_wide, precision=lax.Precision.HIGHEST)
        return update_block(cell_block, gram_sum, cross_sum)
    numbers = jnp.arange(block_total, dtype=jnp.int32)
    renewed = lax.map(one_block, (cell_blocks, lists, counts, numbers))
    return renewed.reshape(cell_major.shape).T
```

```python
import jax
import jax.numpy as jnp
from jax import lax
from jax.sharding import PartitionSpec as P

NS_STEPS = 5
SPAN = 2
LANES = 128


def product(left, right):
    return jnp.dot(left, right, precision=lax.Precision.HIGH)


def row_product(left, right):
    return lax.dot_general(
        left, right, (((1,), (1,)), ((), ())), preferred_element_type=jnp.float32
    )


def listed_rows(index_list, row_total, pool_rows):
    places = jnp.arange(index_list.shape[0], dtype=jnp.int32)
    live = places < row_total
    high = (index_list // LANES)[None, :] == jnp.arange(pool_rows // LANES)[:, None]
    low = (index_list % LANES)[None, :] == jnp.arange(LANES)[:, None]
    marks = row_product(
        (high & live[None, :]).astype(jnp.bfloat16), low.astype(jnp.bfloat16)
    )
    return marks.reshape(1, pool_rows)


def newton_weights(gram_sum, cross_sum):
    members = gram_sum.shape[0]
    identity = jnp.eye(members, dtype=jnp.float32)
    spread = jnp.sqrt(jnp.sum(gram_sum * gram_sum))
    start = 2.0 / (2.0 + spread)
    residual = identity - start * (identity + gram_sum)
    total = identity + residual
    for _ in range(NS_STEPS - 1):
        residual = product(residual, residual)
        total = total + product(total, residual)
    return start * product(total, cross_sum)


def per_device(state, predicted, perturbed, obs_weight, obs_position, row_count, row_index):
    pred = lax.all_to_all(predicted, "member", split_axis=1, concat_axis=0, tiled=True)
    pert = lax.all_to_all(perturbed, "member", split_axis=1, concat_axis=0, tiled=True)
    cells = lax.all_to_all(state, "member", split_axis=1, concat_axis=0, tiled=True)
    groups = lax.axis_size("member")
    group_index = lax.axis_index("member")
    tile_index = lax.axis_index("domain")
    members, pool_rows = pred.shape
    blocks = row_index.shape[1]
    block_cells = cells.shape[1] // blocks
    first_block = (tile_index * groups + group_index) * blocks
    counts = lax.dynamic_index_in_dim(row_count, tile_index, 0, keepdims=False)
    weight = lax.dynamic_slice_in_dim(obs_weight, group_index * pool_rows, pool_rows)[None, :]
    place = lax.dynamic_slice_in_dim(obs_position, group_index * pool_rows, pool_rows)[None, :]
    pred_wide = pred.astype(jnp.float32)
    pred_centred = pred_wide - jnp.mean(pred_wide, axis=0, keepdims=True)
    departure = pert.astype(jnp.float32) - pred_wide
    renewed = []
    for number in range(blocks):
        offset = (place - (first_block + number)).astype(jnp.float32) / SPAN
        marks = listed_rows(row_index[0, number], counts[number], pool_rows)
        factor = marks * (weight * (1.0 / (1.0 + offset * offset)))
        scaled = (factor * pred_centred / jnp.sqrt(members - 1.0)).astype(jnp.bfloat16)
        innovation = (factor * departure).astype(jnp.bfloat16)
        gram_sum = row_product(scaled, scaled)
        cross_sum = row_product(scaled, innovation)
        weights = (newton_weights(gram_sum, cross_sum) / jnp.sqrt(members - 1.0)).astype(
            jnp.bfloat16
        )
        values = cells[:, number * block_cells : (number + 1) * block_cells].astype(jnp.float32)
        centred = (values - jnp.mean(values, axis=0, keepdims=True)).astype(jnp.bfloat16)
        change = lax.dot_general(
            weights, centred, (((0,), (0,)), ((), ())), preferred_element_type=jnp.float32
        )
        renewed.append((values + change).astype(jnp.bfloat16))
    return lax.all_to_all(
        jnp.concatenate(renewed, axis=1), "member", split_axis=0, concat_axis=1, tiled=True
    )


def solution(mesh):
    placed = (
        P("member", "domain"),
        P("member", "domain"),
        P("member", "domain"),
        P("domain"),
        P("domain"),
        P(None, "member"),
        P("domain", "member", None),
    )
    return jax.shard_map(
        per_device, mesh=mesh, in_specs=placed, out_specs=P("member", "domain"), check_vma=False
    )
```

```python
import functools
import math

import jax
import jax.numpy as jnp
from jax import lax
from jax.experimental import pallas as pl
from jax.experimental.pallas import tpu as pltpu
from jax.sharding import PartitionSpec as P

NS_STEPS = 5
SPAN = 2
LANES = 128
CHUNK = 512
F32 = jnp.float32
BF16 = jnp.bfloat16


def row_product(left, right):
    return lax.dot_general(left, right, (((1,), (1,)), ((), ())), preferred_element_type=F32)


def split(value):
    high = value.astype(BF16)
    return high, (value - high.astype(F32)).astype(BF16)


def product(left, right):
    (left_high, left_low), (right_high, right_low) = left, right
    dot = functools.partial(jnp.dot, preferred_element_type=F32)
    return dot(left_high, right_high) + (dot(left_high, right_low) + dot(left_low, right_high))


def peer_order(groups):
    return sorted(range(1, groups), reverse=True)


def kernel(
    groups,
    state,
    predicted,
    perturbed,
    weight_pools,
    place_pools,
    row_count,
    row_index,
    updated,
    pred,
    pert,
    cells,
    renewed,
    weight,
    place,
    factor,
    scaled,
    gram,
    cross,
    residual_high,
    residual_low,
    total,
    inverse_high,
    inverse_low,
    gain,
    send_sem,
    recv_sem,
    own_sem,
    side_sem,
):
    me = lax.axis_index("member")
    tile = lax.axis_index("domain")
    rows_here = pred.shape[1]
    pool_rows = pred.shape[2]
    members = groups * rows_here
    blocks = row_index.shape[1]
    block_cells = cells.shape[3]
    shrink = 1.0 / math.sqrt(members - 1.0)
    peers = peer_order(groups)

    def pool_columns(group):
        return pl.ds(pl.multiple_of(group * pool_rows, pool_rows), pool_rows)

    def cell_columns(group, number):
        return pl.ds(
            pl.multiple_of((group * blocks + number) * block_cells, block_cells), block_cells
        )

    def sources(group):
        return [predicted.at[:, pool_columns(group)], perturbed.at[:, pool_columns(group)]] + [
            state.at[:, cell_columns(group, number)] for number in range(blocks)
        ]

    slots = [pred.at[me], pert.at[me]] + [cells.at[number, me] for number in range(blocks)]
    kinds = len(slots)

    side_copies = [
        pltpu.make_async_copy(weight_pools.at[me], weight, side_sem.at[0]),
        pltpu.make_async_copy(place_pools.at[me], place, side_sem.at[1]),
    ]
    own_copies = [
        pltpu.make_async_copy(source, slot, own_sem.at[kind])
        for kind, (source, slot) in enumerate(zip(sources(me), slots))
    ]
    for copy in side_copies + own_copies:
        copy.start()

    barrier = pltpu.get_barrier_semaphore()
    for step in peers:
        pl.semaphore_signal(
            barrier,
            inc=1,
            device_id=(jnp.bitwise_xor(me, step), tile),
            device_id_type=pl.DeviceIdType.MESH,
        )
    pl.semaphore_wait(barrier, groups - 1)

    def remote(source, target, kind, step):
        return pltpu.make_async_remote_copy(
            src_ref=source,
            dst_ref=target,
            send_sem=send_sem.at[kind, step],
            recv_sem=recv_sem.at[kind, step],
            device_id=(jnp.bitwise_xor(me, step), tile),
            device_id_type=pl.DeviceIdType.MESH,
        )

    incoming = [
        [
            remote(sources(jnp.bitwise_xor(me, step))[kind], slots[kind], kind, step)
            for step in peers
        ]
        for kind in range(kinds)
    ]
    for copies in incoming:
        for copy in copies:
            copy.start()

    def arrived(kind):
        own_copies[kind].wait()
        for copy in incoming[kind]:
            copy.wait_recv()

    for copy in side_copies:
        copy.wait()
    for number in range(blocks):
        first_block = (tile * groups + me) * blocks
        picked = row_index[0, number : number + 1, :]
        length = picked.shape[1]
        live = lax.broadcasted_iota(jnp.int32, (1, length), 1) < row_count[tile, number]
        high = lax.broadcasted_iota(jnp.int32, (pool_rows // LANES, length), 0)
        low = lax.broadcasted_iota(jnp.int32, (LANES, length), 0)
        in_high = jnp.where((high == picked // LANES) & live, 1.0, 0.0).astype(BF16)
        in_low = jnp.where(low == picked % LANES, 1.0, 0.0).astype(BF16)
        marks = row_product(in_high, in_low)
        marks = jnp.concatenate(
            [marks[part : part + 1, :] for part in range(pool_rows // LANES)], axis=1
        )
        offset = (place[...] - (first_block + number)).astype(F32) / SPAN
        factor[number, :, :] = marks * (weight[...] * (1.0 / (1.0 + offset * offset)))

    arrived(0)

    def clear(number):
        gram[number] = jnp.zeros((members, members), F32)
        cross[number] = jnp.zeros((members, members), F32)

    for number in range(blocks):
        clear(number)

    def chunk_columns(chunk):
        return pl.ds(pl.multiple_of(chunk * CHUNK, CHUNK), CHUNK)

    def add_gram(chunk, carry):
        columns = chunk_columns(chunk)
        values = pred[:, :, columns].reshape(members, CHUNK).astype(F32)
        values = values - jnp.sum(values, axis=0, keepdims=True) * (1.0 / members)
        for number in range(blocks):
            rows = (factor[number, :, columns] * values * shrink).astype(BF16)
            scaled[number, :, columns] = rows
            gram[number] += row_product(rows, rows)
        return carry

    lax.fori_loop(0, pool_rows // CHUNK, add_gram, 0)

    def invert(number, carry):
        gram_sum = gram[number]
        squares = jnp.sum(gram_sum * gram_sum, axis=0, keepdims=True)
        spread = jnp.sqrt(jnp.sum(squares, axis=1, keepdims=True))
        start = 2.0 / (2.0 + spread)
        row = lax.broadcasted_iota(jnp.int32, (members, members), 0)
        column = lax.broadcasted_iota(jnp.int32, (members, members), 1)
        identity = jnp.where(row == column, 1.0, 0.0)
        residual = identity - start * (identity + gram_sum)
        total[...] = identity + residual
        residual_high[...], residual_low[...] = split(residual)

        def double(step, carry):
            held = (residual_high[...], residual_low[...])
            held = split(product(held, held))
            residual_high[...], residual_low[...] = held
            total[...] += product(split(total[...]), held)
            return carry

        lax.fori_loop(0, NS_STEPS - 1, double, 0)
        inverse_high[number], inverse_low[number] = split(start * total[...])
        return carry

    lax.fori_loop(0, blocks, invert, 0)

    arrived(1)

    def add_cross(chunk, carry):
        columns = chunk_columns(chunk)
        values = pert[:, :, columns].reshape(members, CHUNK).astype(F32)
        values = values - pred[:, :, columns].reshape(members, CHUNK).astype(F32)
        for number in range(blocks):
            rows = (factor[number, :, columns] * values).astype(BF16)
            cross[number] += row_product(rows, scaled[number, :, columns])
        return carry

    lax.fori_loop(0, pool_rows // CHUNK, add_cross, 0)

    def weigh(number, carry):
        weights = product(split(cross[number]), (inverse_high[number], inverse_low[number]))
        gain[number] = (weights * shrink).astype(BF16)
        return carry

    lax.fori_loop(0, blocks, weigh, 0)

    outgoing = []
    own_out = []
    for number in range(blocks):
        arrived(2 + number)
        values = cells[number].reshape(members, block_cells).astype(F32)
        centred = (values - jnp.sum(values, axis=0, keepdims=True) * (1.0 / members)).astype(BF16)
        change = jnp.dot(gain[number], centred, preferred_element_type=F32)
        renewed[number] = (values + change).astype(BF16).reshape(groups, rows_here, block_cells)
        target = updated.at[:, cell_columns(me, number)]
        for step in peers:
            copy = remote(
                renewed.at[number, jnp.bitwise_xor(me, step)], target, kinds + number, step
            )
            copy.start()
            outgoing.append(copy)
        copy = pltpu.make_async_copy(renewed.at[number, me], target, own_sem.at[kinds + number])
        copy.start()
        own_out.append(copy)

    for copies in incoming:
        for copy in copies:
            copy.wait_send()
    for copy in own_out:
        copy.wait()
    for copy in outgoing:
        copy.wait()


def per_device(groups, state, predicted, perturbed, obs_weight, obs_position, row_count, row_index):
    rows_here, cells_all = state.shape
    pool_rows = predicted.shape[1] // groups
    members = groups * rows_here
    blocks = row_index.shape[1]
    block_cells = cells_all // groups // blocks
    kinds = 2 + 2 * blocks
    anywhere = pl.BlockSpec(memory_space=pl.ANY)
    square = (blocks, members, members)
    return pl.pallas_call(
        functools.partial(kernel, groups),
        out_shape=jax.ShapeDtypeStruct(state.shape, state.dtype),
        in_specs=[anywhere] * 5
        + [pl.BlockSpec(memory_space=pltpu.SMEM), pl.BlockSpec(memory_space=pltpu.VMEM)],
        out_specs=anywhere,
        scratch_shapes=[
            pltpu.VMEM((groups, rows_here, pool_rows), BF16),
            pltpu.VMEM((groups, rows_here, pool_rows), BF16),
            pltpu.VMEM((blocks, groups, rows_here, block_cells), BF16),
            pltpu.VMEM((blocks, groups, rows_here, block_cells), BF16),
            pltpu.VMEM((1, pool_rows), F32),
            pltpu.VMEM((1, pool_rows), jnp.int32),
            pltpu.VMEM((blocks, 1, pool_rows), F32),
            pltpu.VMEM((blocks, members, pool_rows), BF16),
            pltpu.VMEM(square, F32),
            pltpu.VMEM(square, F32),
            pltpu.VMEM((members, members), BF16),
            pltpu.VMEM((members, members), BF16),
            pltpu.VMEM((members, members), F32),
            pltpu.VMEM(square, BF16),
            pltpu.VMEM(square, BF16),
            pltpu.VMEM(square, BF16),
            pltpu.SemaphoreType.DMA((kinds, groups)),
            pltpu.SemaphoreType.DMA((kinds, groups)),
            pltpu.SemaphoreType.DMA((kinds,)),
            pltpu.SemaphoreType.DMA((2,)),
        ],
        compiler_params=pltpu.CompilerParams(
            collective_id=0, has_side_effects=True, vmem_limit_bytes=56 * 2**20
        ),
    )(
        state,
        predicted,
        perturbed,
        obs_weight.reshape(groups, 1, pool_rows),
        obs_position.reshape(groups, 1, pool_rows),
        row_count,
        row_index,
    )


def solution(mesh):
    placed = (
        P("member", "domain"),
        P("member", "domain"),
        P("member", "domain"),
        P("domain"),
        P("domain"),
        P(None, "member"),
        P("domain", "member", None),
    )
    return jax.shard_map(
        functools.partial(per_device, mesh.shape["member"]),
        mesh=mesh,
        in_specs=placed,
        out_specs=P("member", "domain"),
        check_vma=False,
    )
```

```python
import functools
import math

import jax
import jax.numpy as jnp
from jax import lax
from jax.experimental import pallas as pl
from jax.experimental.pallas import tpu as pltpu
from jax.sharding import PartitionSpec as P

NS_STEPS = 5
SPAN = 2
LANES = 128
CHUNK = 512
F32 = jnp.float32
BF16 = jnp.bfloat16


def row_product(left, right):
    return lax.dot_general(left, right, (((1,), (1,)), ((), ())), preferred_element_type=F32)


def split(value):
    high = value.astype(BF16)
    return high, (value - high.astype(F32)).astype(BF16)


def product(left, right):
    (left_high, left_low), (right_high, right_low) = left, right
    dot = functools.partial(jnp.dot, preferred_element_type=F32)
    return dot(left_high, right_high) + (dot(left_high, right_low) + dot(left_low, right_high))


def send_orders(groups):
    near_first = list(range(1, groups))
    far_first = near_first[groups // 2 - 1 :] + near_first[: groups // 2 - 1]
    return list(zip(near_first, far_first))


def kernel(
    groups,
    state,
    predicted,
    perturbed,
    weight_pools,
    place_pools,
    row_count,
    row_index,
    updated,
    counts,
    lists,
    pred,
    pert,
    cells,
    renewed,
    weight,
    place,
    factor,
    scaled,
    gram,
    cross,
    residual_high,
    residual_low,
    total,
    inverse_high,
    inverse_low,
    gain,
    send_sem,
    recv_sem,
    own_sem,
    side_sem,
):
    me = lax.axis_index("member")
    tile = lax.axis_index("domain")
    rows_here = pred.shape[1]
    pool_rows = pred.shape[2]
    members = groups * rows_here
    blocks = row_index.shape[1]
    block_cells = cells.shape[3]
    shrink = 1.0 / math.sqrt(members - 1.0)
    peers = list(range(1, groups))
    orders = send_orders(groups)

    def pool_columns(group):
        return pl.ds(pl.multiple_of(group * pool_rows, pool_rows), pool_rows)

    def cell_columns(group, number):
        return pl.ds(
            pl.multiple_of((group * blocks + number) * block_cells, block_cells), block_cells
        )

    def sources(group):
        return [predicted.at[:, pool_columns(group)], perturbed.at[:, pool_columns(group)]] + [
            state.at[:, cell_columns(group, number)] for number in range(blocks)
        ]

    slots = [pred.at[me], pert.at[me]] + [cells.at[number, me] for number in range(blocks)]
    kinds = len(slots)

    side_copies = [
        pltpu.make_async_copy(weight_pools.at[me], weight, side_sem.at[0]),
        pltpu.make_async_copy(place_pools.at[me], place, side_sem.at[1]),
        pltpu.make_async_copy(row_count, counts, side_sem.at[2]),
        pltpu.make_async_copy(row_index, lists, side_sem.at[3]),
    ]
    own_copies = [
        pltpu.make_async_copy(source, slot, own_sem.at[kind])
        for kind, (source, slot) in enumerate(zip(sources(me), slots))
    ]
    barrier = pltpu.get_barrier_semaphore()
    for step in peers:
        pl.semaphore_signal(
            barrier,
            inc=1,
            device_id=(jnp.bitwise_xor(me, step), tile),
            device_id_type=pl.DeviceIdType.MESH,
        )
    for copy in side_copies + own_copies:
        copy.start()
    pl.semaphore_wait(barrier, groups - 1)

    def remote(source, target, kind, step):
        return pltpu.make_async_remote_copy(
            src_ref=source,
            dst_ref=target,
            send_sem=send_sem.at[kind, step],
            recv_sem=recv_sem.at[kind, step],
            device_id=(jnp.bitwise_xor(me, step), tile),
            device_id_type=pl.DeviceIdType.MESH,
        )

    incoming = [
        [
            remote(sources(jnp.bitwise_xor(me, step))[kind], slots[kind], kind, step)
            for step in peers
        ]
        for kind in range(kinds)
    ]
    def chosen(order):
        return order[0] + (order[1] - order[0]) * (tile % 2)

    for kind in range(kinds):
        for order in orders:
            step = chosen(order)
            remote(sources(jnp.bitwise_xor(me, step))[kind], slots[kind], kind, step).start()

    def arrived(kind):
        own_copies[kind].wait()
        for copy in incoming[kind]:
            copy.wait_recv()

    for copy in side_copies:
        copy.wait()
    for number in range(blocks):
        first_block = (tile * groups + me) * blocks
        picked = lists[0, number : number + 1, :]
        length = picked.shape[1]
        live = lax.broadcasted_iota(jnp.int32, (1, length), 1) < counts[tile, number]
        high = lax.broadcasted_iota(jnp.int32, (pool_rows // LANES, length), 0)
        low = lax.broadcasted_iota(jnp.int32, (LANES, length), 0)
        in_high = jnp.where((high == picked // LANES) & live, 1.0, 0.0).astype(BF16)
        in_low = jnp.where(low == picked % LANES, 1.0, 0.0).astype(BF16)
        marks = row_product(in_high, in_low)
        marks = jnp.concatenate(
            [marks[part : part + 1, :] for part in range(pool_rows // LANES)], axis=1
        )
        offset = (place[...] - (first_block + number)).astype(F32) / SPAN
        factor[number, :, :] = marks * (weight[...] * (1.0 / (1.0 + offset * offset)))

    arrived(0)

    def clear(number):
        gram[number] = jnp.zeros((members, members), F32)
        cross[number] = jnp.zeros((members, members), F32)

    for number in range(blocks):
        clear(number)

    def chunk_columns(chunk):
        return pl.ds(pl.multiple_of(chunk * CHUNK, CHUNK), CHUNK)

    def add_gram(chunk, carry):
        columns = chunk_columns(chunk)
        values = pred[:, :, columns].reshape(members, CHUNK).astype(F32)
        values = values - jnp.sum(values, axis=0, keepdims=True) * (1.0 / members)
        for number in range(blocks):
            rows = (factor[number, :, columns] * values * shrink).astype(BF16)
            scaled[number, :, columns] = rows
            gram[number] += row_product(rows, rows)
        return carry

    lax.fori_loop(0, pool_rows // CHUNK, add_gram, 0)

    def invert(number, carry):
        gram_sum = gram[number]
        squares = jnp.sum(gram_sum * gram_sum, axis=0, keepdims=True)
        spread = jnp.sqrt(jnp.sum(squares, axis=1, keepdims=True))
        start = 2.0 / (2.0 + spread)
        row = lax.broadcasted_iota(jnp.int32, (members, members), 0)
        column = lax.broadcasted_iota(jnp.int32, (members, members), 1)
        identity = jnp.where(row == column, 1.0, 0.0)
        residual = identity - start * (identity + gram_sum)
        total[...] = identity + residual
        residual_high[...], residual_low[...] = split(residual)

        def double(step, carry):
            held = (residual_high[...], residual_low[...])
            held = split(product(held, held))
            residual_high[...], residual_low[...] = held
            total[...] += product(split(total[...]), held)
            return carry

        lax.fori_loop(0, NS_STEPS - 1, double, 0)
        inverse_high[number], inverse_low[number] = split(start * total[...])
        return carry

    lax.fori_loop(0, blocks, invert, 0)

    arrived(1)

    def add_cross(chunk, carry):
        columns = chunk_columns(chunk)
        values = pert[:, :, columns].reshape(members, CHUNK).astype(F32)
        values = values - pred[:, :, columns].reshape(members, CHUNK).astype(F32)
        for number in range(blocks):
            rows = (factor[number, :, columns] * values).astype(BF16)
            cross[number] += row_product(rows, scaled[number, :, columns])
        return carry

    lax.fori_loop(0, pool_rows // CHUNK, add_cross, 0)

    def weigh(number, carry):
        weights = product(split(cross[number]), (inverse_high[number], inverse_low[number]))
        gain[number] = (weights * shrink).astype(BF16)
        return carry

    lax.fori_loop(0, blocks, weigh, 0)

    outgoing = []
    own_out = []
    for number in range(blocks):
        arrived(2 + number)
        values = cells[number].reshape(members, block_cells).astype(F32)
        centred = (values - jnp.sum(values, axis=0, keepdims=True) * (1.0 / members)).astype(BF16)
        change = jnp.dot(gain[number], centred, preferred_element_type=F32)
        renewed[number] = (values + change).astype(BF16).reshape(groups, rows_here, block_cells)
        target = updated.at[:, cell_columns(me, number)]

        def give(step, number=number, target=target):
            return remote(
                renewed.at[number, jnp.bitwise_xor(me, step)], target, kinds + number, step
            )

        for order in orders:
            give(chosen(order)).start()
        outgoing += [give(step) for step in peers]
        copy = pltpu.make_async_copy(renewed.at[number, me], target, own_sem.at[kinds + number])
        copy.start()
        own_out.append(copy)

    for copies in incoming:
        for copy in copies:
            copy.wait_send()
    for copy in own_out:
        copy.wait()
    for copy in outgoing:
        copy.wait()


def per_device(groups, state, predicted, perturbed, obs_weight, obs_position, row_count, row_index):
    rows_here, cells_all = state.shape
    pool_rows = predicted.shape[1] // groups
    members = groups * rows_here
    blocks = row_index.shape[1]
    block_cells = cells_all // groups // blocks
    kinds = 2 + 2 * blocks
    anywhere = pl.BlockSpec(memory_space=pl.ANY)
    square = (blocks, members, members)
    return pl.pallas_call(
        functools.partial(kernel, groups),
        out_shape=jax.ShapeDtypeStruct(state.shape, state.dtype),
        in_specs=[anywhere] * 7,
        out_specs=anywhere,
        scratch_shapes=[
            pltpu.SMEM(row_count.shape, jnp.int32),
            pltpu.VMEM(row_index.shape, jnp.int32),
            pltpu.VMEM((groups, rows_here, pool_rows), BF16),
            pltpu.VMEM((groups, rows_here, pool_rows), BF16),
            pltpu.VMEM((blocks, groups, rows_here, block_cells), BF16),
            pltpu.VMEM((blocks, groups, rows_here, block_cells), BF16),
            pltpu.VMEM((1, pool_rows), F32),
            pltpu.VMEM((1, pool_rows), jnp.int32),
            pltpu.VMEM((blocks, 1, pool_rows), F32),
            pltpu.VMEM((blocks, members, pool_rows), BF16),
            pltpu.VMEM(square, F32),
            pltpu.VMEM(square, F32),
            pltpu.VMEM((members, members), BF16),
            pltpu.VMEM((members, members), BF16),
            pltpu.VMEM((members, members), F32),
            pltpu.VMEM(square, BF16),
            pltpu.VMEM(square, BF16),
            pltpu.VMEM(square, BF16),
            pltpu.SemaphoreType.DMA((kinds, groups)),
            pltpu.SemaphoreType.DMA((kinds, groups)),
            pltpu.SemaphoreType.DMA((kinds,)),
            pltpu.SemaphoreType.DMA((4,)),
        ],
        compiler_params=pltpu.CompilerParams(
            collective_id=0, has_side_effects=True, vmem_limit_bytes=56 * 2**20
        ),
    )(
        state,
        predicted,
        perturbed,
        obs_weight.reshape(groups, 1, pool_rows),
        obs_position.reshape(groups, 1, pool_rows),
        row_count,
        row_index,
    )


def solution(mesh):
    placed = (
        P("member", "domain"),
        P("member", "domain"),
        P("member", "domain"),
        P("domain"),
        P("domain"),
        P(None, "member"),
        P("domain", "member", None),
    )
    return jax.shard_map(
        functools.partial(per_device, mesh.shape["member"]),
        mesh=mesh,
        in_specs=placed,
        out_specs=P("member", "domain"),
        check_vma=False,
    )
```

```python
import functools
import math

import jax
import jax.numpy as jnp
from jax import lax
from jax.experimental import pallas as pl
from jax.experimental.pallas import tpu as pltpu
from jax.sharding import PartitionSpec as P

NS_STEPS = 5
SPAN = 2
LANES = 128
CHUNK = 512
F32 = jnp.float32
BF16 = jnp.bfloat16


def row_product(left, right):
    return lax.dot_general(left, right, (((1,), (1,)), ((), ())), preferred_element_type=F32)


def split(value):
    high = value.astype(BF16)
    return high, (value - high.astype(F32)).astype(BF16)


def product(left, right):
    (left_high, left_low), (right_high, right_low) = left, right
    dot = functools.partial(jnp.dot, preferred_element_type=F32)
    return dot(left_high, right_high) + (dot(left_high, right_low) + dot(left_low, right_high))


def send_orders(groups, done=()):
    near_first = [step for step in range(1, groups) if step not in done]
    far_first = [step for step in near_first if step >= groups // 2]
    far_first += [step for step in near_first if step < groups // 2]
    return list(zip(near_first, far_first))


def doublings(groups):
    return [1 << bit for bit in range(groups.bit_length() - 1)]


def kernel(
    groups,
    state,
    predicted,
    perturbed,
    weight_pools,
    place_pools,
    row_count,
    row_index,
    updated,
    counts,
    lists,
    pred,
    pert,
    cells,
    renewed,
    weight,
    place,
    factor,
    scaled,
    gram,
    cross,
    residual_high,
    residual_low,
    total,
    inverse_high,
    inverse_low,
    gain,
    send_sem,
    recv_sem,
    own_sem,
    side_sem,
    meet_sem,
):
    me = lax.axis_index("member")
    tile = lax.axis_index("domain")
    rows_here = pred.shape[1]
    pool_rows = pred.shape[2]
    members = groups * rows_here
    blocks = row_index.shape[1]
    block_cells = cells.shape[3]
    shrink = 1.0 / math.sqrt(members - 1.0)
    peers = list(range(1, groups))
    orders = send_orders(groups)

    def pool_columns(group):
        return pl.ds(pl.multiple_of(group * pool_rows, pool_rows), pool_rows)

    def cell_columns(group, number):
        return pl.ds(
            pl.multiple_of((group * blocks + number) * block_cells, block_cells), block_cells
        )

    def sources(group):
        return [predicted.at[:, pool_columns(group)], perturbed.at[:, pool_columns(group)]] + [
            state.at[:, cell_columns(group, number)] for number in range(blocks)
        ]

    slots = [pred.at[me], pert.at[me]] + [cells.at[number, me] for number in range(blocks)]
    kinds = len(slots)

    side_copies = [
        pltpu.make_async_copy(weight_pools.at[me], weight, side_sem.at[0]),
        pltpu.make_async_copy(place_pools.at[me], place, side_sem.at[1]),
        pltpu.make_async_copy(row_count, counts, side_sem.at[2]),
        pltpu.make_async_copy(row_index, lists, side_sem.at[3]),
    ]
    own_copies = [
        pltpu.make_async_copy(source, slot, own_sem.at[kind])
        for kind, (source, slot) in enumerate(zip(sources(me), slots))
    ]
    barrier = pltpu.get_barrier_semaphore()
    partners = doublings(groups)[::-1]

    def greet(semaphore, step):
        pl.semaphore_signal(
            semaphore,
            inc=1,
            device_id=(jnp.bitwise_xor(me, step), tile),
            device_id_type=pl.DeviceIdType.MESH,
        )

    for step in partners:
        greet(barrier, step)
    for copy in side_copies + own_copies:
        copy.start()
    pl.semaphore_wait(barrier, len(partners))

    def remote(source, target, kind, step):
        return pltpu.make_async_remote_copy(
            src_ref=source,
            dst_ref=target,
            send_sem=send_sem.at[kind, step],
            recv_sem=recv_sem.at[kind, step],
            device_id=(jnp.bitwise_xor(me, step), tile),
            device_id_type=pl.DeviceIdType.MESH,
        )

    incoming = [
        [
            remote(sources(jnp.bitwise_xor(me, step))[kind], slots[kind], kind, step)
            for step in peers
        ]
        for kind in range(kinds)
    ]
    def chosen(order):
        return order[0] + (order[1] - order[0]) * (tile % 2)

    def send(kind, step):
        remote(sources(jnp.bitwise_xor(me, step))[kind], slots[kind], kind, step).start()

    for step in partners:
        send(0, step)
    for number, step in enumerate(partners):
        greet(meet_sem.at[number], step)
        pl.semaphore_wait(meet_sem.at[number], 1)
    for order in send_orders(groups, partners):
        send(0, chosen(order))
    for kind in range(1, kinds):
        for order in orders:
            send(kind, chosen(order))

    def arrived(kind):
        own_copies[kind].wait()
        for copy in incoming[kind]:
            copy.wait_recv()

    for copy in side_copies:
        copy.wait()
    for number in range(blocks):
        first_block = (tile * groups + me) * blocks
        picked = lists[0, number : number + 1, :]
        length = picked.shape[1]
        live = lax.broadcasted_iota(jnp.int32, (1, length), 1) < counts[tile, number]
        high = lax.broadcasted_iota(jnp.int32, (pool_rows // LANES, length), 0)
        low = lax.broadcasted_iota(jnp.int32, (LANES, length), 0)
        in_high = jnp.where((high == picked // LANES) & live, 1.0, 0.0).astype(BF16)
        in_low = jnp.where(low == picked % LANES, 1.0, 0.0).astype(BF16)
        marks = row_product(in_high, in_low)
        marks = jnp.concatenate(
            [marks[part : part + 1, :] for part in range(pool_rows // LANES)], axis=1
        )
        offset = (place[...] - (first_block + number)).astype(F32) / SPAN
        factor[number, :, :] = marks * (weight[...] * (1.0 / (1.0 + offset * offset)))

    arrived(0)

    def clear(number):
        gram[number] = jnp.zeros((members, members), F32)
        cross[number] = jnp.zeros((members, members), F32)

    for number in range(blocks):
        clear(number)

    def chunk_columns(chunk):
        return pl.ds(pl.multiple_of(chunk * CHUNK, CHUNK), CHUNK)

    def add_gram(chunk, carry):
        columns = chunk_columns(chunk)
        values = pred[:, :, columns].reshape(members, CHUNK).astype(F32)
        values = values - jnp.sum(values, axis=0, keepdims=True) * (1.0 / members)
        for number in range(blocks):
            rows = (factor[number, :, columns] * values * shrink).astype(BF16)
            scaled[number, :, columns] = rows
            gram[number] += row_product(rows, rows)
        return carry

    lax.fori_loop(0, pool_rows // CHUNK, add_gram, 0)

    def invert(number, carry):
        gram_sum = gram[number]
        squares = jnp.sum(gram_sum * gram_sum, axis=0, keepdims=True)
        spread = jnp.sqrt(jnp.sum(squares, axis=1, keepdims=True))
        start = 2.0 / (2.0 + spread)
        row = lax.broadcasted_iota(jnp.int32, (members, members), 0)
        column = lax.broadcasted_iota(jnp.int32, (members, members), 1)
        identity = jnp.where(row == column, 1.0, 0.0)
        residual = identity - start * (identity + gram_sum)
        total[...] = identity + residual
        residual_high[...], residual_low[...] = split(residual)

        def double(step, carry):
            held = (residual_high[...], residual_low[...])
            held = split(product(held, held))
            residual_high[...], residual_low[...] = held
            total[...] += product(split(total[...]), held)
            return carry

        lax.fori_loop(0, NS_STEPS - 1, double, 0)
        inverse_high[number], inverse_low[number] = split(start * total[...])
        return carry

    lax.fori_loop(0, blocks, invert, 0)

    arrived(1)

    def add_cross(chunk, carry):
        columns = chunk_columns(chunk)
        values = pert[:, :, columns].reshape(members, CHUNK).astype(F32)
        values = values - pred[:, :, columns].reshape(members, CHUNK).astype(F32)
        for number in range(blocks):
            rows = (factor[number, :, columns] * values).astype(BF16)
            cross[number] += row_product(rows, scaled[number, :, columns])
        return carry

    lax.fori_loop(0, pool_rows // CHUNK, add_cross, 0)

    def weigh(number, carry):
        weights = product(split(cross[number]), (inverse_high[number], inverse_low[number]))
        gain[number] = (weights * shrink).astype(BF16)
        return carry

    lax.fori_loop(0, blocks, weigh, 0)

    outgoing = []
    own_out = []
    for number in range(blocks):
        arrived(2 + number)
        values = cells[number].reshape(members, block_cells).astype(F32)
        centred = (values - jnp.sum(values, axis=0, keepdims=True) * (1.0 / members)).astype(BF16)
        change = jnp.dot(gain[number], centred, preferred_element_type=F32)
        renewed[number] = (values + change).astype(BF16).reshape(groups, rows_here, block_cells)
        target = updated.at[:, cell_columns(me, number)]

        def give(step, number=number, target=target):
            return remote(
                renewed.at[number, jnp.bitwise_xor(me, step)], target, kinds + number, step
            )

        for order in orders:
            give(chosen(order)).start()
        outgoing += [give(step) for step in peers]
        copy = pltpu.make_async_copy(renewed.at[number, me], target, own_sem.at[kinds + number])
        copy.start()
        own_out.append(copy)

    for copies in incoming:
        for copy in copies:
            copy.wait_send()
    for copy in own_out:
        copy.wait()
    for copy in outgoing:
        copy.wait()


def per_device(groups, state, predicted, perturbed, obs_weight, obs_position, row_count, row_index):
    rows_here, cells_all = state.shape
    pool_rows = predicted.shape[1] // groups
    members = groups * rows_here
    blocks = row_index.shape[1]
    block_cells = cells_all // groups // blocks
    kinds = 2 + 2 * blocks
    anywhere = pl.BlockSpec(memory_space=pl.ANY)
    square = (blocks, members, members)
    return pl.pallas_call(
        functools.partial(kernel, groups),
        out_shape=jax.ShapeDtypeStruct(state.shape, state.dtype),
        in_specs=[anywhere] * 7,
        out_specs=anywhere,
        scratch_shapes=[
            pltpu.SMEM(row_count.shape, jnp.int32),
            pltpu.VMEM(row_index.shape, jnp.int32),
            pltpu.VMEM((groups, rows_here, pool_rows), BF16),
            pltpu.VMEM((groups, rows_here, pool_rows), BF16),
            pltpu.VMEM((blocks, groups, rows_here, block_cells), BF16),
            pltpu.VMEM((blocks, groups, rows_here, block_cells), BF16),
            pltpu.VMEM((1, pool_rows), F32),
            pltpu.VMEM((1, pool_rows), jnp.int32),
            pltpu.VMEM((blocks, 1, pool_rows), F32),
            pltpu.VMEM((blocks, members, pool_rows), BF16),
            pltpu.VMEM(square, F32),
            pltpu.VMEM(square, F32),
            pltpu.VMEM((members, members), BF16),
            pltpu.VMEM((members, members), BF16),
            pltpu.VMEM((members, members), F32),
            pltpu.VMEM(square, BF16),
            pltpu.VMEM(square, BF16),
            pltpu.VMEM(square, BF16),
            pltpu.SemaphoreType.DMA((kinds, groups)),
            pltpu.SemaphoreType.DMA((kinds, groups)),
            pltpu.SemaphoreType.DMA((kinds,)),
            pltpu.SemaphoreType.DMA((4,)),
            pltpu.SemaphoreType.REGULAR((len(doublings(groups)),)),
        ],
        compiler_params=pltpu.CompilerParams(
            collective_id=0, has_side_effects=True, vmem_limit_bytes=56 * 2**20
        ),
    )(
        state,
        predicted,
        perturbed,
        obs_weight.reshape(groups, 1, pool_rows),
        obs_position.reshape(groups, 1, pool_rows),
        row_count,
        row_index,
    )


def solution(mesh):
    placed = (
        P("member", "domain"),
        P("member", "domain"),
        P("member", "domain"),
        P("domain"),
        P("domain"),
        P(None, "member"),
        P("domain", "member", None),
    )
    return jax.shard_map(
        functools.partial(per_device, mesh.shape["member"]),
        mesh=mesh,
        in_specs=placed,
        out_specs=P("member", "domain"),
        check_vma=False,
    )
```
